512 devices in a mesh: src: 32 (over x, y, z_hi), rcv: 16 (over z_lo, core).
Axes of the slice: x: 4, y: 4, z: 16 (z_hi: 2, z_lo: 8; z = z_hi * 8 + z_lo), core: 2. Of those that a mesh axis runs over, the one named last changes fastest.
Arguments:
- observed: bfloat16 [32, 1280, 128, 128], P('src', 'rcv'), may hold values from -6 to 6
- block_row: int32 [32, 1280], P('src', 'rcv'), may hold values from 0 to 31, as said below
- block_col: int32 [32, 1280], P('src', 'rcv'), may hold values from 0 to 15
- live: int32 [32, 16], P('src', 'rcv'), may hold values from 20 to 80, as said below
- row_factor: bfloat16 [131072, 64], P('src'), may hold values from -5 to 5
- col_factor: bfloat16 [32768, 64], P('rcv'), may hold values from -5 to 5
Outputs:
- new_rows: bfloat16 [131072, 64], P('src')
- new_cols: bfloat16 [32768, 64], P('rcv')
The draws below stay inside these ranges and needn't reach their ends.
Inputs may be any that keep to these rules, and one draw needn't show every extreme that they name: `block_row`: within one device the 80 slots name distinct blocks of its tile. `live`: some device has all 80 slots in use.
All inputs are finite; a program needn't handle non-finite values.
Results may differ from the reference program's by a relative error of at most 0.007.
Values may be sent and summed in bfloat16 or wider, within the bound.
A program may use at most 64 MiB of HBM per device.

```python
import math
import jax
import jax.numpy as jnp
from jax import lax

BLK = 128
RANK = 64
SB = 32
CB = 16
CAP = 80
NS = 131072
NR = 32768
ROWSPAN = 5120
COLSPAN = 20480
N_SRC = 32
N_RCV = 16


def pick_blocks(device_key):
    return jax.random.permutation(device_key, SB * CB)[:CAP]


def draw_slot_ids(key):
    folded = jax.random.fold_in(key, 11)
    device_keys = jax.random.split(folded, N_SRC * N_RCV)
    picks = jax.vmap(pick_blocks)(device_keys)
    return picks.astype(jnp.int32)


def draw_block_row(key, part):
    slot_ids = draw_slot_ids(key)
    return (slot_ids // CB).reshape(N_SRC, N_RCV * CAP).astype(jnp.int32)


def draw_block_col(key, part):
    slot_ids = draw_slot_ids(key)
    return (slot_ids % CB).reshape(N_SRC, N_RCV * CAP).astype(jnp.int32)


def draw_live(key, part):
    base_counts = jax.random.randint(jax.random.fold_in(key, 13), (N_SRC * N_RCV,), max(1, CAP // 4), CAP - CAP // 4 + 1)
    full_device = jax.random.randint(jax.random.fold_in(key, 17), (), 0, N_SRC * N_RCV)
    counts = jnp.where(jnp.arange(N_SRC * N_RCV) == full_device, CAP, base_counts)
    return counts.reshape(N_SRC, N_RCV).astype(jnp.int32)


def steps_of(rng, dims, pieces, low, largest):
    factor_of, own = 1.0, jax.random.fold_in(rng, 6)
    for dim, blocks in pieces:
        draws = jnp.exp(jax.random.uniform(jax.random.fold_in(own, dim), (blocks,), jnp.float32, low / len(pieces), largest / len(pieces)))
        factor_of = factor_of * jnp.repeat(draws, dims[dim] // blocks).reshape([-1 if axis == dim else 1 for axis in range(len(dims))])
    return factor_of


def normal_values(stream_key, extent, spread, most, shards=(), kind=jnp.bfloat16):
    array = jax.random.normal(stream_key, extent, jnp.float32) * spread
    if len(shards) > 0:
        array = steps_of(stream_key, extent, shards, -0.22, 0.18) * array
    return jnp.clip(array, min=-most, max=most).astype(kind)


def setup_inputs(seed: int = 0) -> dict:
    seeds = jax.random.split(jax.random.key(seed), 7)
    return {
        "observed": normal_values(seeds[0], (N_SRC, N_RCV * CAP, BLK, BLK), 1.0, 6.0, ((0, 32), (1, 16))),
        "block_row": draw_block_row(jax.random.fold_in(seeds[6], 71), 0),
        "block_col": draw_block_col(jax.random.fold_in(seeds[6], 71), 0),
        "live": draw_live(jax.random.fold_in(seeds[6], 71), 0),
        "row_factor": normal_values(seeds[4], (NS, RANK), 0.35, 5.0, ((0, 32),)),
        "col_factor": normal_values(seeds[5], (NR, RANK), 0.35, 5.0, ((0, 16),)),
    }


def device_terms(row_tile, col_tile, slot_data, rows_id, cols_id, slot_count):
    row_table = row_tile.reshape(SB, BLK, RANK).astype(jnp.float32)
    col_table = col_tile.reshape(CB, BLK, RANK).astype(jnp.float32)
    row_pick = (rows_id[:, None] == jnp.arange(SB, dtype=jnp.int32)[None, :]).astype(jnp.float32)
    col_pick = (cols_id[:, None] == jnp.arange(CB, dtype=jnp.int32)[None, :]).astype(jnp.float32)
    row_blocks = jnp.einsum('ks,sar->kar', row_pick, row_table)
    col_blocks = jnp.einsum('kc,cbr->kbr', col_pick, col_table)
    predicted = jnp.einsum('kar,kbr->kab', row_blocks, col_blocks)
    slot_live = jnp.arange(CAP, dtype=jnp.int32) < slot_count
    residual = jnp.where(slot_live[:, None, None], predicted - slot_data.astype(jnp.float32), 0.0)
    residual = residual.astype(jnp.bfloat16).astype(jnp.float32)
    row_terms = jnp.einsum('kab,kbr->kar', residual, col_blocks)
    col_terms = jnp.einsum('kab,kar->kbr', residual, row_blocks)
    row_grad = jnp.einsum('ks,kar->sar', row_pick, row_terms).reshape(SB * BLK, RANK)
    col_grad = jnp.einsum('kc,kbr->cbr', col_pick, col_terms).reshape(CB * BLK, RANK)
    return (row_grad, col_grad)

def reference(observed, block_row, block_col, live, row_factor, col_factor):
    device_total = N_SRC * N_RCV
    all_data = observed.reshape(device_total, CAP, BLK, BLK)
    all_rows = block_row.reshape(device_total, CAP)
    all_cols = block_col.reshape(device_total, CAP)
    all_live = live.reshape(device_total)

    def visit(carry, inputs):
        row_acc, col_acc = carry
        device_index, slot_data, rows_id, cols_id, slot_count = inputs
        src_index = (device_index // N_RCV).astype(jnp.int32)
        rcv_index = (device_index % N_RCV).astype(jnp.int32)
        row_start = (src_index * (SB * BLK)).astype(jnp.int32)
        col_start = (rcv_index * (CB * BLK)).astype(jnp.int32)
        row_tile = lax.dynamic_slice_in_dim(row_factor, row_start, SB * BLK, 0)
        col_tile = lax.dynamic_slice_in_dim(col_factor, col_start, CB * BLK, 0)
        row_grad, col_grad = device_terms(row_tile, col_tile, slot_data, rows_id, cols_id, slot_count)
        old_rows = lax.dynamic_slice_in_dim(row_acc, row_start, SB * BLK, 0)
        row_acc = lax.dynamic_update_slice_in_dim(row_acc, old_rows + row_grad, row_start, 0)
        old_cols = lax.dynamic_slice_in_dim(col_acc, col_start, CB * BLK, 0)
        col_acc = lax.dynamic_update_slice_in_dim(col_acc, old_cols + col_grad, col_start, 0)
        return ((row_acc, col_acc), None)
    start_carry = (jnp.zeros((NS, RANK), jnp.float32), jnp.zeros((NR, RANK), jnp.float32))
    device_ids = jnp.arange(device_total, dtype=jnp.int32)
    (row_sums, col_sums), _ = lax.scan(visit, start_carry, (device_ids, all_data, all_rows, all_cols, all_live))
    row_step = 0.5 / math.sqrt(ROWSPAN)
    col_step = 0.5 / math.sqrt(COLSPAN)
    new_rows = (0.9 * row_factor.astype(jnp.float32) - row_step * row_sums).astype(jnp.bfloat16)
    new_cols = (0.9 * col_factor.astype(jnp.float32) - col_step * col_sums).astype(jnp.bfloat16)
    return (new_rows, new_cols)
```

```python
import functools
import math

import jax
import jax.numpy as jnp
from jax import lax
from jax.experimental import pallas as pl
from jax.experimental.pallas import tpu as pltpu
from jax.sharding import PartitionSpec as P

MESH = pl.DeviceIdType.MESH
F32 = jnp.float32
BF16 = jnp.bfloat16

BLK = 128
GROUP = 8
XN, YN, ZH = 4, 4, 2
QUAD = 4


def dot(a, b, dims):
    return lax.dot_general(a, b, (dims, ((), ())), preferred_element_type=F32)


def terms_kernel(
    brow, bcol, live, obs_hbm, row_t, col_t, row_out, col_out, row_own, col_own,
    obs, row_tab, row_acc, col_acc, sems,
):
    slots = obs.shape[0]
    n_row, n_col = row_acc.shape[0], col_acc.shape[0]

    def fetch(g):
        part = pl.ds(g * GROUP, GROUP)
        return pltpu.make_async_copy(obs_hbm.at[part], obs.at[part], sems.at[g])

    for g in range(slots // GROUP):
        fetch(g).start()
    row_acc[...] = jnp.zeros_like(row_acc)
    col_acc[...] = jnp.zeros_like(col_acc)
    for i in range(n_row):
        row_tab[i] = row_t[:, i * BLK : (i + 1) * BLK].T
    count = live[0, 0]

    def group(g, carry):
        fetch(g).wait()

        @pl.when(g * GROUP < count)
        def _():
            terms = []
            for u in range(GROUP):
                k = g * GROUP + u
                i, j = brow[0, k], bcol[0, k]
                ct = col_t[:, pl.ds(pl.multiple_of(j * BLK, BLK), BLK)]
                rt = row_t[:, pl.ds(pl.multiple_of(i * BLK, BLK), BLK)]
                pred = dot(row_tab[i], ct, ((1,), (0,)))
                res = pred - obs[k].astype(F32)
                res = jnp.where(k < count, res, 0.0).astype(BF16)
                terms.append((i, j, dot(ct, res, ((1,), (1,))), dot(rt, res, ((1,), (0,)))))
            for i, j, row_term, col_term in terms:
                row_acc[i] += row_term
                col_acc[j] += col_term

        return carry

    lax.fori_loop(0, slots // GROUP, group, 0)
    row_out[...] = row_acc[...].astype(BF16)
    col_out[...] = col_acc[...].astype(BF16)

    src, rcv = lax.axis_index("src"), lax.axis_index("rcv")
    mine = rcv % 2 * (n_row // 2) + rcv // 2 * 2
    for u in range(2):
        part = pl.ds(pl.multiple_of((mine + u) * BLK, BLK), BLK)
        row_own[u] = 0.9 * row_t[:, part].astype(F32)
    part = pl.ds(pl.multiple_of(src // ZH * BLK, BLK), BLK)
    col_own[0] = 0.9 * col_t[:, part].astype(F32)


def sum_kernel(
    row_step, col_step, row_in, col_in, row_own, col_own, row_out, col_out,
    core_buf, far_sum, near_sum, far_buf, near_buf, far_send, far_recv, col_buf, col_send, col_recv,
    send_sems, recv_sems,
):
    src, rcv = lax.axis_index("src"), lax.axis_index("rcv")
    x, y, zh = src // (YN * ZH), src // ZH % YN, src % ZH
    z, c = rcv // 2, rcv % 2
    q, p = z // QUAD, z % QUAD
    b = src // ZH
    half = row_in.shape[0] // 2
    qb = half // 2

    def at(zz, cc):
        return (src, zz * 2 + cc)

    core = at(z, 1 - c)
    far_z = (1 - q) * QUAD + p
    far = at(far_z, c)
    up = [q * QUAD + (p + d) % QUAD for d in range(1, QUAD)]
    down = [(p + QUAD - d) % QUAD for d in range(1, QUAD)]
    mates = [at(m, c) for m in up]
    steps = [(dx, dy) for dx in range(XN) for dy in range(YN) if dx or dy]
    steps.sort(key=lambda s: -(min(s[0], XN - s[0]) + min(s[1], YN - s[1])))
    places = [(x + dx) % XN * YN + (y + dy) % YN for dx, dy in steps]
    peers = [(place * ZH + zh, rcv) for place in places]
    twin = (b * ZH + 1 - zh, rcv)

    barrier = pltpu.get_barrier_semaphore()
    everyone = [core, far, twin] + mates + peers
    for device in everyone:
        pl.semaphore_signal(barrier, inc=1, device_id=device, device_id_type=MESH)
    pl.semaphore_wait(barrier, len(everyone))

    sent = []

    def copy(source, target, number, device):
        return pltpu.make_async_remote_copy(
            src_ref=source, dst_ref=target, send_sem=send_sems.at[number], recv_sem=recv_sems.at[number],
            device_id=device, device_id_type=MESH,
        )

    def send(source, target, number, device):
        one = copy(source, target, number, device)
        one.start()
        sent.append(one)

    def arrive(target, number):
        copy(target, target, number, core).wait_recv()

    CORE, FAR_IN, NEAR_IN, FAR, COL_IN, TWIN, NEAR_OUT, FAR_OUT, RELAY, CORE_OUT, COL_OUT = (
        0, 2, 5, 8, 9, 24, 25, 28, 29, 32, 40,
    )

    for k, quad in enumerate((1 - q, q)):
        send(row_in.at[pl.ds((1 - c) * half + quad * qb, qb)], core_buf.at[k], CORE + k, core)
    for k, (place, peer) in enumerate(zip(places, peers)):
        send(col_in.at[place], col_buf.at[k], COL_IN + k, peer)

    for k, (quad, total, buf, number) in enumerate(
        ((1 - q, far_sum, far_buf, FAR_IN), (q, near_sum, near_buf, NEAR_IN))
    ):
        arrive(core_buf.at[k], CORE + k)
        own = row_in[pl.ds(c * half + quad * qb, qb)].astype(F32)
        total[...] = (own + core_buf[k].astype(F32)).astype(BF16)
        for d in range(QUAD - 1):
            send(total.at[pl.ds((p + d + 1) % QUAD * 2, 2)], buf.at[d], number + d, mates[d])

    acc = far_sum[pl.ds(p * 2, 2)].astype(F32)
    for d in range(QUAD - 1):
        arrive(far_buf.at[d], FAR_IN + d)
        acc += far_buf[d].astype(F32)
    far_send[...] = acc.astype(BF16)
    send(far_send, far_recv, FAR, far)

    acc = col_in[b].astype(F32)
    for k in range(len(peers)):
        arrive(col_buf.at[k], COL_IN + k)
        acc += col_buf[k].astype(F32)
    col_send[...] = acc.astype(BF16)
    send(col_send, col_recv, TWIN, twin)

    acc = near_sum[pl.ds(p * 2, 2)].astype(F32)
    for d in range(QUAD - 1):
        arrive(near_buf.at[d], NEAR_IN + d)
        acc += near_buf[d].astype(F32)
    arrive(far_recv, FAR)
    acc += far_recv[...].astype(F32)

    def blocks(zz, cc):
        return row_out.at[pl.ds(cc * half + zz * 2, 2)]

    mine = blocks(z, c)
    mine[...] = (row_own[...] - row_step * acc).astype(BF16)
    send(mine, mine, FAR_OUT, far)
    for d in range(QUAD - 1):
        send(mine, mine, NEAR_OUT + d, mates[d])
    send(mine, mine, CORE_OUT, core)

    arrive(col_recv, TWIN)
    acc = col_send[...].astype(F32) + col_recv[...].astype(F32)
    col_out[b] = (col_own[0] - col_step * acc).astype(BF16)
    for k, peer in enumerate(peers):
        send(col_out.at[b], col_out.at[b], COL_OUT + k, peer)

    theirs = blocks(far_z, c)
    arrive(theirs, FAR_OUT)
    for d in range(QUAD - 1):
        send(theirs, theirs, RELAY + d, mates[d])
    send(theirs, theirs, CORE_OUT + 1, core)
    spots = [z, far_z]
    for quad, number in ((q, NEAR_OUT), (1 - q, RELAY)):
        for d in range(QUAD - 1):
            spot = quad * QUAD + down[d]
            part = blocks(spot, c)
            arrive(part, number + d)
            send(part, part, CORE_OUT + len(spots), core)
            spots.append(spot)
    for k, (dx, dy) in enumerate(steps):
        place = (x + XN - dx) % XN * YN + (y + YN - dy) % YN
        arrive(col_out.at[place], COL_OUT + k)
    for k, spot in enumerate(spots):
        arrive(blocks(spot, 1 - c), CORE_OUT + k)
    for one in sent:
        one.wait_send()


def local(observed, block_row, block_col, live, row_factor, col_factor):
    slot_data = observed[0]
    slots = slot_data.shape[0]
    rank = row_factor.shape[1]
    n_row, n_col = row_factor.shape[0] // BLK, col_factor.shape[0] // BLK
    row_t, col_t = row_factor.T, col_factor.T
    vmem = pl.BlockSpec(memory_space=pltpu.VMEM)
    smem = pl.BlockSpec(memory_space=pltpu.SMEM)

    row_terms, col_terms, row_own, col_own = pl.pallas_call(
        terms_kernel,
        out_shape=(
            jax.ShapeDtypeStruct((n_row, rank, BLK), BF16),
            jax.ShapeDtypeStruct((n_col, rank, BLK), BF16),
            jax.ShapeDtypeStruct((2, rank, BLK), F32),
            jax.ShapeDtypeStruct((1, rank, BLK), F32),
        ),
        in_specs=[smem, smem, smem, pl.BlockSpec(memory_space=pl.ANY), vmem, vmem],
        out_specs=(vmem,) * 4,
        scratch_shapes=[
            pltpu.VMEM((slots, BLK, BLK), BF16),
            pltpu.VMEM((n_row, BLK, rank), BF16),
            pltpu.VMEM((n_row, rank, BLK), F32),
            pltpu.VMEM((n_col, rank, BLK), F32),
            pltpu.SemaphoreType.DMA((slots // GROUP,)),
        ],
        name="terms",
    )(block_row, block_col, live, slot_data, row_t, col_t)

    row_step = 0.5 / math.sqrt(slots * BLK * lax.axis_size("rcv") // n_row)
    col_step = 0.5 / math.sqrt(slots * BLK * lax.axis_size("src") // n_col)
    copies = 55
    new_rows, new_cols = pl.pallas_call(
        functools.partial(sum_kernel, row_step, col_step),
        out_shape=(
            jax.ShapeDtypeStruct((n_row, rank, BLK), BF16),
            jax.ShapeDtypeStruct((n_col, rank, BLK), BF16),
        ),
        in_specs=[vmem] * 4,
        out_specs=(vmem, vmem),
        scratch_shapes=[
            pltpu.VMEM((2, n_row // 4, rank, BLK), BF16),
            pltpu.VMEM((n_row // 4, rank, BLK), BF16),
            pltpu.VMEM((n_row // 4, rank, BLK), BF16),
            pltpu.VMEM((QUAD - 1, 2, rank, BLK), BF16),
            pltpu.VMEM((QUAD - 1, 2, rank, BLK), BF16),
            pltpu.VMEM((2, rank, BLK), BF16),
            pltpu.VMEM((2, rank, BLK), BF16),
            pltpu.VMEM((XN * YN - 1, rank, BLK), BF16),
            pltpu.VMEM((rank, BLK), BF16),
            pltpu.VMEM((rank, BLK), BF16),
            pltpu.SemaphoreType.DMA((copies,)),
            pltpu.SemaphoreType.DMA((copies,)),
        ],
        compiler_params=pltpu.CompilerParams(collective_id=0, has_side_effects=True),
        name="sums",
    )(row_terms, col_terms, row_own, col_own)

    def whole(blocks):
        return blocks.transpose(1, 0, 2).reshape(rank, -1).T

    return whole(new_rows), whole(new_cols)


def solution(mesh):
    return jax.shard_map(
        local,
        mesh=mesh,
        in_specs=(
            P("src", "rcv", None, None),
            P("src", "rcv"),
            P("src", "rcv"),
            P("src", "rcv"),
            P("src", None),
            P("rcv", None),
        ),
        out_specs=(P("src", None), P("rcv", None)),
        check_vma=False,
    )
```

```python
import functools
import math

import jax
import jax.numpy as jnp
from jax import lax
from jax.experimental import pallas as pl
from jax.experimental.pallas import tpu as pltpu
from jax.sharding import PartitionSpec as P

MESH = pl.DeviceIdType.MESH
F32 = jnp.float32
BF16 = jnp.bfloat16

BLK = 128
TERMS_LIMIT = 55_200_000
LIMIT = 16 << 20
GROUP = 16
XN, YN, ZH = 4, 4, 2
QUAD = 4


def dot(a, b, dims):
    return lax.dot_general(a, b, (dims, ((), ())), preferred_element_type=F32)


def terms_kernel(
    brow_hbm, bcol_hbm, live, obs_hbm, row_hbm, col_hbm, row_out, col_out, row_own, col_own,
    brow, bcol, row_t, col_t, obs, row_tab, row_acc, col_acc, arg_sems, sems,
):
    slots = obs.shape[0]
    n_row, n_col = row_acc.shape[0], col_acc.shape[0]

    args = [
        pltpu.make_async_copy(source, target, arg_sems.at[k])
        for k, (source, target) in enumerate(
            ((brow_hbm, brow), (bcol_hbm, bcol), (row_hbm, row_t), (col_hbm, col_t))
        )
    ]

    def fetch(g):
        part = pl.ds(g * GROUP, GROUP)
        return pltpu.make_async_copy(obs_hbm.at[part], obs.at[part], sems.at[g])

    for arg in args:
        arg.start()
    for g in range(slots // GROUP):
        fetch(g).start()
    row_acc[...] = jnp.zeros_like(row_acc)
    col_acc[...] = jnp.zeros_like(col_acc)
    for arg in args:
        arg.wait()
    for i in range(n_row):
        row_tab[i] = row_t[:, i * BLK : (i + 1) * BLK].T
    count = live[0, 0]

    def pick(k):
        i, j = brow[0, k], bcol[0, k]
        rt = row_t[:, pl.ds(pl.multiple_of(i * BLK, BLK), BLK)]
        ct = col_t[:, pl.ds(pl.multiple_of(j * BLK, BLK), BLK)]
        return i, j, rt, ct

    def group(g, carry):
        fetch(g).wait()

        @pl.when(g * GROUP < count)
        def _():
            for u in range(GROUP):
                k = g * GROUP + u
                i, _, _, ct = pick(k)
                res = dot(row_tab[i], ct, ((1,), (0,))) - obs[k].astype(F32)
                obs[k] = jnp.where(k < count, res, 0.0).astype(BF16)
            terms = []
            for u in range(GROUP):
                k = g * GROUP + u
                i, j, rt, ct = pick(k)
                res = obs[k]
                terms.append((i, j, dot(ct, res, ((1,), (1,))), dot(rt, res, ((1,), (0,)))))
            for i, j, row_term, col_term in terms:
                row_acc[i] += row_term
                col_acc[j] += col_term

        return carry

    lax.fori_loop(0, slots // GROUP, group, 0)
    row_out[...] = row_acc[...].astype(BF16)
    col_out[...] = col_acc[...].astype(BF16)

    src, rcv = lax.axis_index("src"), lax.axis_index("rcv")
    mine = rcv % 2 * (n_row // 2) + rcv // 2 * 2
    for u in range(2):
        part = pl.ds(pl.multiple_of((mine + u) * BLK, BLK), BLK)
        row_own[u] = 0.9 * row_t[:, part].astype(F32)
    part = pl.ds(pl.multiple_of(src // ZH * BLK, BLK), BLK)
    col_own[0] = 0.9 * col_t[:, part].astype(F32)


def sum_kernel(
    row_step, col_step, row_in, col_in, row_own, col_own, row_out, col_out,
    core_buf, far_sum, near_sum, far_buf, near_buf, far_send, far_recv, col_buf, col_send, col_recv,
    twin_in, send_sems, recv_sems,
):
    src, rcv = lax.axis_index("src"), lax.axis_index("rcv")
    x, y, zh = src // (YN * ZH), src // ZH % YN, src % ZH
    z, c = rcv // 2, rcv % 2
    q, p = z // QUAD, z % QUAD
    b = src // ZH
    half = row_in.shape[0] // 2
    qb = half // 2

    def at(zz, cc):
        return (src, zz * 2 + cc)

    core = at(z, 1 - c)
    far_z = (1 - q) * QUAD + p
    far = at(far_z, c)
    up = [q * QUAD + (p + d) % QUAD for d in range(1, QUAD)]
    down = [(p + QUAD - d) % QUAD for d in range(1, QUAD)]
    mates = [at(m, c) for m in up]
    steps = [(dx, dy) for dx in range(XN) for dy in range(YN) if dx or dy]
    steps.sort(key=lambda s: -(min(s[0], XN - s[0]) + min(s[1], YN - s[1])))
    places = [(x + dx) % XN * YN + (y + dy) % YN for dx, dy in steps]
    peers = [(place * ZH + zh, rcv) for place in places]
    twin = (b * ZH + 1 - zh, rcv)
    side = (b * ZH + 1 - zh, far_z * 2 + c)

    barrier = pltpu.get_barrier_semaphore()
    everyone = [core, far, side] + mates + peers
    for device in everyone:
        pl.semaphore_signal(barrier, inc=1, device_id=device, device_id_type=MESH)
    pl.semaphore_wait(barrier, len(everyone))
    pl.semaphore_signal(twin_in, inc=1, device_id=far, device_id_type=MESH)

    sent = []

    def copy(source, target, number, device):
        return pltpu.make_async_remote_copy(
            src_ref=source, dst_ref=target, send_sem=send_sems.at[number], recv_sem=recv_sems.at[number],
            device_id=device, device_id_type=MESH,
        )

    def send(source, target, number, device):
        one = copy(source, target, number, device)
        one.start()
        sent.append(one)

    def arrive(target, number):
        copy(target, target, number, core).wait_recv()

    CORE, FAR_IN, NEAR_IN, FAR, COL_IN, TWIN, NEAR_OUT, FAR_OUT, RELAY, CORE_OUT, COL_OUT = (
        0, 2, 5, 8, 9, 24, 25, 28, 29, 32, 40,
    )

    for k, quad in enumerate((1 - q, q)):
        send(row_in.at[pl.ds((1 - c) * half + quad * qb, qb)], core_buf.at[k], CORE + k, core)
    for k, (place, peer) in enumerate(zip(places, peers)):
        send(col_in.at[place], col_buf.at[k], COL_IN + k, peer)

    for k, (quad, total, buf, number) in enumerate(
        ((1 - q, far_sum, far_buf, FAR_IN), (q, near_sum, near_buf, NEAR_IN))
    ):
        arrive(core_buf.at[k], CORE + k)
        own = row_in[pl.ds(c * half + quad * qb, qb)].astype(F32)
        total[...] = (own + core_buf[k].astype(F32)).astype(BF16)
        for d in range(QUAD - 1):
            send(total.at[pl.ds((p + d + 1) % QUAD * 2, 2)], buf.at[d], number + d, mates[d])

    acc = far_sum[pl.ds(p * 2, 2)].astype(F32)
    for d in range(QUAD - 1):
        arrive(far_buf.at[d], FAR_IN + d)
        acc += far_buf[d].astype(F32)
    far_send[...] = acc.astype(BF16)
    send(far_send, far_recv, FAR, far)

    acc = col_in[b].astype(F32)
    for k in range(len(peers)):
        arrive(col_buf.at[k], COL_IN + k)
        acc += col_buf[k].astype(F32)
    col_send[...] = acc.astype(BF16)
    pl.semaphore_wait(twin_in, 1)
    send(col_send, col_recv, TWIN, twin)

    acc = near_sum[pl.ds(p * 2, 2)].astype(F32)
    for d in range(QUAD - 1):
        arrive(near_buf.at[d], NEAR_IN + d)
        acc += near_buf[d].astype(F32)
    arrive(far_recv, FAR)
    acc += far_recv[...].astype(F32)

    def blocks(zz, cc):
        return row_out.at[pl.ds(cc * half + zz * 2, 2)]

    mine = blocks(z, c)
    mine[...] = (row_own[...] - row_step * acc).astype(BF16)
    send(mine, mine, FAR_OUT, far)
    for d in range(QUAD - 1):
        send(mine, mine, NEAR_OUT + d, mates[d])
    send(mine, mine, CORE_OUT, core)

    arrive(col_recv, TWIN)
    acc = col_send[...].astype(F32) + col_recv[...].astype(F32)
    col_out[b] = (col_own[0] - col_step * acc).astype(BF16)
    for k, peer in enumerate(peers):
        send(col_out.at[b], col_out.at[b], COL_OUT + k, peer)

    theirs = blocks(far_z, c)
    arrive(theirs, FAR_OUT)
    for d in range(QUAD - 1):
        send(theirs, theirs, RELAY + d, mates[d])
    send(theirs, theirs, CORE_OUT + 1, core)
    spots = [z, far_z]
    for quad, number in ((q, NEAR_OUT), (1 - q, RELAY)):
        for d in range(QUAD - 1):
            spot = quad * QUAD + down[d]
            part = blocks(spot, c)
            arrive(part, number + d)
            send(part, part, CORE_OUT + len(spots), core)
            spots.append(spot)
    for k, (dx, dy) in enumerate(steps):
        place = (x + XN - dx) % XN * YN + (y + YN - dy) % YN
        arrive(col_out.at[place], COL_OUT + k)
    for k, spot in enumerate(spots):
        arrive(blocks(spot, 1 - c), CORE_OUT + k)
    for one in sent:
        one.wait_send()


def local(observed, block_row, block_col, live, row_factor, col_factor):
    slot_data = observed[0]
    slots = slot_data.shape[0]
    rank = row_factor.shape[1]
    n_row, n_col = row_factor.shape[0] // BLK, col_factor.shape[0] // BLK
    row_t, col_t = row_factor.T, col_factor.T
    vmem = pl.BlockSpec(memory_space=pltpu.VMEM)
    hbm = pl.BlockSpec(memory_space=pl.ANY)

    row_terms, col_terms, row_own, col_own = pl.pallas_call(
        terms_kernel,
        out_shape=(
            jax.ShapeDtypeStruct((n_row, rank, BLK), BF16),
            jax.ShapeDtypeStruct((n_col, rank, BLK), BF16),
            jax.ShapeDtypeStruct((2, rank, BLK), F32),
            jax.ShapeDtypeStruct((1, rank, BLK), F32),
        ),
        in_specs=[hbm, hbm, pl.BlockSpec(memory_space=pltpu.SMEM), hbm, hbm, hbm],
        out_specs=(vmem,) * 4,
        scratch_shapes=[
            pltpu.SMEM((1, slots), jnp.int32),
            pltpu.SMEM((1, slots), jnp.int32),
            pltpu.VMEM((rank, n_row * BLK), BF16),
            pltpu.VMEM((rank, n_col * BLK), BF16),
            pltpu.VMEM((slots, BLK, BLK), BF16),
            pltpu.VMEM((n_row, BLK, rank), BF16),
            pltpu.VMEM((n_row, rank, BLK), F32),
            pltpu.VMEM((n_col, rank, BLK), F32),
            pltpu.SemaphoreType.DMA((4,)),
            pltpu.SemaphoreType.DMA((slots // GROUP,)),
        ],
        compiler_params=pltpu.CompilerParams(vmem_limit_bytes=TERMS_LIMIT),
        name="terms",
    )(block_row, block_col, live, slot_data, row_t, col_t)

    row_step = 0.5 / math.sqrt(slots * BLK * lax.axis_size("rcv") // n_row)
    col_step = 0.5 / math.sqrt(slots * BLK * lax.axis_size("src") // n_col)
    copies = 55
    new_rows, new_cols = pl.pallas_call(
        functools.partial(sum_kernel, row_step, col_step),
        out_shape=(
            jax.ShapeDtypeStruct((n_row, rank, BLK), BF16),
            jax.ShapeDtypeStruct((n_col, rank, BLK), BF16),
        ),
        in_specs=[vmem] * 4,
        out_specs=(vmem, vmem),
        scratch_shapes=[
            pltpu.VMEM((2, n_row // 4, rank, BLK), BF16),
            pltpu.VMEM((n_row // 4, rank, BLK), BF16),
            pltpu.VMEM((n_row // 4, rank, BLK), BF16),
            pltpu.VMEM((QUAD - 1, 2, rank, BLK), BF16),
            pltpu.VMEM((QUAD - 1, 2, rank, BLK), BF16),
            pltpu.VMEM((2, rank, BLK), BF16),
            pltpu.VMEM((2, rank, BLK), BF16),
            pltpu.VMEM((XN * YN - 1, rank, BLK), BF16),
            pltpu.VMEM((rank, BLK), BF16),
            pltpu.VMEM((rank, BLK), BF16),
            pltpu.SemaphoreType.REGULAR,
            pltpu.SemaphoreType.DMA((copies,)),
            pltpu.SemaphoreType.DMA((copies,)),
        ],
        compiler_params=pltpu.CompilerParams(
            collective_id=0, has_side_effects=True, vmem_limit_bytes=LIMIT
        ),
        name="sums",
    )(row_terms, col_terms, row_own, col_own)

    def whole(blocks):
        return blocks.transpose(1, 0, 2).reshape(rank, -1).T

    return whole(new_rows), whole(new_cols)


def solution(mesh):
    return jax.shard_map(
        local,
        mesh=mesh,
        in_specs=(
            P("src", "rcv", None, None),
            P("src", "rcv"),
            P("src", "rcv"),
            P("src", "rcv"),
            P("src", None),
            P("rcv", None),
        ),
        out_specs=(P("src", None), P("rcv", None)),
        check_vma=False,
    )
```

```python
import functools
import math

import jax
import jax.numpy as jnp
from jax import lax
from jax.experimental import pallas as pl
from jax.experimental.pallas import tpu as pltpu
from jax.sharding import PartitionSpec as P

MESH = pl.DeviceIdType.MESH
F32 = jnp.float32
BF16 = jnp.bfloat16

BLK = 128
LIMIT = 16 << 20
GROUP = 16
XN, YN, ZH = 4, 4, 2
QUAD = 4


def dot(a, b, dims):
    return lax.dot_general(a, b, (dims, ((), ())), preferred_element_type=F32)


def terms_kernel(
    brow_hbm, bcol_hbm, live, obs_hbm, row_hbm, col_hbm, row_out, col_out, row_own, col_own,
    brow, bcol, row_t, col_t, obs, row_tab, row_acc, col_acc, arg_sems, sems,
):
    slots = obs.shape[0]
    n_row, n_col = row_acc.shape[0], col_acc.shape[0]

    args = [
        pltpu.make_async_copy(source, target, arg_sems.at[k])
        for k, (source, target) in enumerate(
            ((brow_hbm, brow), (bcol_hbm, bcol), (row_hbm, row_t), (col_hbm, col_t))
        )
    ]

    def fetch(g):
        part = pl.ds(g * GROUP, GROUP)
        return pltpu.make_async_copy(obs_hbm.at[part], obs.at[part], sems.at[g])

    for arg in args:
        arg.start()
    for g in range(slots // GROUP):
        fetch(g).start()
    row_acc[...] = jnp.zeros_like(row_acc)
    col_acc[...] = jnp.zeros_like(col_acc)
    for arg in args:
        arg.wait()
    for i in range(n_row):
        row_tab[i] = row_t[:, i * BLK : (i + 1) * BLK].T
    count = live[0, 0]

    def pick(k):
        i, j = brow[0, k], bcol[0, k]
        rt = row_t[:, pl.ds(pl.multiple_of(i * BLK, BLK), BLK)]
        ct = col_t[:, pl.ds(pl.multiple_of(j * BLK, BLK), BLK)]
        return i, j, rt, ct

    def group(g, carry):
        fetch(g).wait()

        @pl.when(g * GROUP < count)
        def _():
            for u in range(GROUP):
                k = g * GROUP + u
                i, _, _, ct = pick(k)
                res = dot(row_tab[i], ct, ((1,), (0,))) - obs[k].astype(F32)
                obs[k] = jnp.where(k < count, res, 0.0).astype(BF16)
            terms = []
            for u in range(GROUP):
                k = g * GROUP + u
                i, j, rt, ct = pick(k)
                res = obs[k]
                terms.append((i, j, dot(ct, res, ((1,), (1,))), dot(rt, res, ((1,), (0,)))))
            for i, j, row_term, col_term in terms:
                row_acc[i] += row_term
                col_acc[j] += col_term

        return carry

    lax.fori_loop(0, slots // GROUP, group, 0)
    row_out[...] = row_acc[...].astype(BF16)
    col_out[...] = col_acc[...].astype(BF16)

    src, rcv = lax.axis_index("src"), lax.axis_index("rcv")
    mine = rcv % 2 * (n_row // 2) + rcv // 2 * 2
    for u in range(2):
        part = pl.ds(pl.multiple_of((mine + u) * BLK, BLK), BLK)
        row_own[u] = 0.9 * row_t[:, part].astype(F32)
    part = pl.ds(pl.multiple_of(src // ZH * BLK, BLK), BLK)
    col_own[0] = 0.9 * col_t[:, part].astype(F32)


def sum_kernel(
    row_step, col_step, row_in, col_in, row_own, col_own, row_out, col_out,
    core_buf, far_sum, near_sum, far_buf, near_buf, far_send, far_recv, col_buf, col_send, col_recv,
    twin_in, send_sems, recv_sems,
):
    src, rcv = lax.axis_index("src"), lax.axis_index("rcv")
    x, y, zh = src // (YN * ZH), src // ZH % YN, src % ZH
    z, c = rcv // 2, rcv % 2
    q, p = z // QUAD, z % QUAD
    b = src // ZH
    half = row_in.shape[0] // 2
    qb = half // 2

    def at(zz, cc):
        return (src, zz * 2 + cc)

    core = at(z, 1 - c)
    far_z = (1 - q) * QUAD + p
    far = at(far_z, c)
    up = [q * QUAD + (p + d) % QUAD for d in range(1, QUAD)]
    down = [(p + QUAD - d) % QUAD for d in range(1, QUAD)]
    mates = [at(m, c) for m in up]
    steps = [(dx, dy) for dx in range(XN) for dy in range(YN) if dx or dy]
    steps.sort(key=lambda s: -(min(s[0], XN - s[0]) + min(s[1], YN - s[1])))
    places = [(x + dx) % XN * YN + (y + dy) % YN for dx, dy in steps]
    peers = [(place * ZH + zh, rcv) for place in places]
    twin = (b * ZH + 1 - zh, rcv)
    side = (b * ZH + 1 - zh, far_z * 2 + c)

    barrier = pltpu.get_barrier_semaphore()
    everyone = [core, far, side] + mates + peers
    for device in everyone:
        pl.semaphore_signal(barrier, inc=1, device_id=device, device_id_type=MESH)
    pl.semaphore_wait(barrier, len(everyone))
    pl.semaphore_signal(twin_in, inc=1, device_id=far, device_id_type=MESH)

    sent = []

    def copy(source, target, number, device):
        return pltpu.make_async_remote_copy(
            src_ref=source, dst_ref=target, send_sem=send_sems.at[number], recv_sem=recv_sems.at[number],
            device_id=device, device_id_type=MESH,
        )

    def send(source, target, number, device):
        one = copy(source, target, number, device)
        one.start()
        sent.append(one)
        return one

    def leave(ones):
        for one in ones:
            one.wait_send()
        sent[:] = [one for one in sent if not any(one is other for other in ones)]

    def arrive(target, number):
        copy(target, target, number, core).wait_recv()

    CORE_FAR, CORE_NEAR, FAR_IN, NEAR_IN, FAR, COL_IN, TWIN = 0, 4, 5, 8, 11, 12, 27
    NEAR_OUT, FAR_OUT, RELAY, CORE_OUT, COL_OUT = 28, 31, 32, 35, 43

    for d in range(QUAD):
        spot = (1 - q) * QUAD + (p + d + 1) % QUAD
        send(row_in.at[pl.ds((1 - c) * half + spot * 2, 2)], core_buf.at[0, pl.ds(d * 2, 2)], CORE_FAR + d, core)
    send(row_in.at[pl.ds((1 - c) * half + q * qb, qb)], core_buf.at[1], CORE_NEAR, core)
    for k, (place, peer) in enumerate(zip(places, peers)):
        send(col_in.at[place], col_buf.at[k], COL_IN + k, peer)

    first = []
    for d in range(QUAD):
        part = pl.ds(d * 2, 2)
        spot = (1 - q) * QUAD + (p + d + 1) % QUAD
        arrive(core_buf.at[0, part], CORE_FAR + d)
        own = row_in[pl.ds(c * half + spot * 2, 2)].astype(F32)
        far_sum[part] = (own + core_buf[0, part].astype(F32)).astype(BF16)
        if d < QUAD - 1:
            first.append(send(far_sum.at[part], far_buf.at[d], FAR_IN + d, mates[d]))
    arrive(core_buf.at[1], CORE_NEAR)
    own = row_in[pl.ds(c * half + q * qb, qb)].astype(F32)
    near_sum[...] = (own + core_buf[1].astype(F32)).astype(BF16)
    leave(first)
    for d in range(QUAD - 1):
        send(near_sum.at[pl.ds((p + d + 1) % QUAD * 2, 2)], near_buf.at[d], NEAR_IN + d, mates[d])

    acc = far_sum[pl.ds(QUAD * 2 - 2, 2)].astype(F32)
    for d in range(QUAD - 1):
        arrive(far_buf.at[d], FAR_IN + d)
        acc += far_buf[d].astype(F32)
    far_send[...] = acc.astype(BF16)
    send(far_send, far_recv, FAR, far)

    acc = col_in[b].astype(F32)
    for k in range(len(peers)):
        arrive(col_buf.at[k], COL_IN + k)
        acc += col_buf[k].astype(F32)
    col_send[...] = acc.astype(BF16)
    pl.semaphore_wait(twin_in, 1)
    send(col_send, col_recv, TWIN, twin)

    acc = near_sum[pl.ds(p * 2, 2)].astype(F32)
    for d in range(QUAD - 1):
        arrive(near_buf.at[d], NEAR_IN + d)
        acc += near_buf[d].astype(F32)
    arrive(far_recv, FAR)
    acc += far_recv[...].astype(F32)

    def blocks(zz, cc):
        return row_out.at[pl.ds(cc * half + zz * 2, 2)]

    mine = blocks(z, c)
    mine[...] = (row_own[...] - row_step * acc).astype(BF16)
    leave([send(mine, mine, FAR_OUT, far)])
    for d in range(QUAD - 1):
        send(mine, mine, NEAR_OUT + d, mates[d])
    send(mine, mine, CORE_OUT, core)

    arrive(col_recv, TWIN)
    acc = col_send[...].astype(F32) + col_recv[...].astype(F32)
    col_out[b] = (col_own[0] - col_step * acc).astype(BF16)
    for k, peer in enumerate(peers):
        send(col_out.at[b], col_out.at[b], COL_OUT + k, peer)

    theirs = blocks(far_z, c)
    arrive(theirs, FAR_OUT)
    for d in range(QUAD - 1):
        send(theirs, theirs, RELAY + d, mates[d])
    send(theirs, theirs, CORE_OUT + 1, core)
    spots = [z, far_z]
    for quad, number in ((q, NEAR_OUT), (1 - q, RELAY)):
        for d in range(QUAD - 1):
            spot = quad * QUAD + down[d]
            part = blocks(spot, c)
            arrive(part, number + d)
            send(part, part, CORE_OUT + len(spots), core)
            spots.append(spot)
    for k, (dx, dy) in enumerate(steps):
        place = (x + XN - dx) % XN * YN + (y + YN - dy) % YN
        arrive(col_out.at[place], COL_OUT + k)
    for k, spot in enumerate(spots):
        arrive(blocks(spot, 1 - c), CORE_OUT + k)
    for one in sent:
        one.wait_send()


def local(observed, block_row, block_col, live, row_factor, col_factor):
    slot_data = observed[0]
    slots = slot_data.shape[0]
    rank = row_factor.shape[1]
    n_row, n_col = row_factor.shape[0] // BLK, col_factor.shape[0] // BLK
    row_t, col_t = row_factor.T, col_factor.T
    vmem = pl.BlockSpec(memory_space=pltpu.VMEM)
    hbm = pl.BlockSpec(memory_space=pl.ANY)

    fixed = functools.partial(pltpu.with_memory_space_constraint, memory_space=pltpu.HBM)
    row_terms, col_terms, row_own, col_own = pl.pallas_call(
        terms_kernel,
        out_shape=(
            jax.ShapeDtypeStruct((n_row, rank, BLK), BF16),
            jax.ShapeDtypeStruct((n_col, rank, BLK), BF16),
            jax.ShapeDtypeStruct((2, rank, BLK), F32),
            jax.ShapeDtypeStruct((1, rank, BLK), F32),
        ),
        in_specs=[hbm, hbm, pl.BlockSpec(memory_space=pltpu.SMEM), hbm, hbm, hbm],
        out_specs=(vmem,) * 4,
        scratch_shapes=[
            pltpu.SMEM((1, slots), jnp.int32),
            pltpu.SMEM((1, slots), jnp.int32),
            pltpu.VMEM((rank, n_row * BLK), BF16),
            pltpu.VMEM((rank, n_col * BLK), BF16),
            pltpu.VMEM((slots, BLK, BLK), BF16),
            pltpu.VMEM((n_row, BLK, rank), BF16),
            pltpu.VMEM((n_row, rank, BLK), F32),
            pltpu.VMEM((n_col, rank, BLK), F32),
            pltpu.SemaphoreType.DMA((4,)),
            pltpu.SemaphoreType.DMA((slots // GROUP,)),
        ],
        compiler_params=pltpu.CompilerParams(vmem_limit_bytes=LIMIT),
        name="terms",
    )(fixed(block_row), fixed(block_col), live, fixed(slot_data), fixed(row_t), fixed(col_t))

    row_step = 0.5 / math.sqrt(slots * BLK * lax.axis_size("rcv") // n_row)
    col_step = 0.5 / math.sqrt(slots * BLK * lax.axis_size("src") // n_col)
    copies = 58
    new_rows, new_cols = pl.pallas_call(
        functools.partial(sum_kernel, row_step, col_step),
        out_shape=(
            jax.ShapeDtypeStruct((n_row, rank, BLK), BF16),
            jax.ShapeDtypeStruct((n_col, rank, BLK), BF16),
        ),
        in_specs=[vmem] * 4,
        out_specs=(vmem, vmem),
        scratch_shapes=[
            pltpu.VMEM((2, n_row // 4, rank, BLK), BF16),
            pltpu.VMEM((n_row // 4, rank, BLK), BF16),
            pltpu.VMEM((n_row // 4, rank, BLK), BF16),
            pltpu.VMEM((QUAD - 1, 2, rank, BLK), BF16),
            pltpu.VMEM((QUAD - 1, 2, rank, BLK), BF16),
            pltpu.VMEM((2, rank, BLK), BF16),
            pltpu.VMEM((2, rank, BLK), BF16),
            pltpu.VMEM((XN * YN - 1, rank, BLK), BF16),
            pltpu.VMEM((rank, BLK), BF16),
            pltpu.VMEM((rank, BLK), BF16),
            pltpu.SemaphoreType.REGULAR,
            pltpu.SemaphoreType.DMA((copies,)),
            pltpu.SemaphoreType.DMA((copies,)),
        ],
        compiler_params=pltpu.CompilerParams(
            collective_id=0, has_side_effects=True, vmem_limit_bytes=LIMIT
        ),
        name="sums",
    )(row_terms, col_terms, row_own, col_own)

    def whole(blocks):
        return blocks.transpose(1, 0, 2).reshape(rank, -1).T

    return whole(new_rows), whole(new_cols)


def solution(mesh):
    return jax.shard_map(
        local,
        mesh=mesh,
        in_specs=(
            P("src", "rcv", None, None),
            P("src", "rcv"),
            P("src", "rcv"),
            P("src", "rcv"),
            P("src", None),
            P("rcv", None),
        ),
        out_specs=(P("src", None), P("rcv", None)),
        check_vma=False,
    )
```

```python
import functools
import math

import jax
import jax.numpy as jnp
from jax import lax
from jax.experimental import pallas as pl
from jax.experimental.pallas import tpu as pltpu
from jax.sharding import PartitionSpec as P

MESH = pl.DeviceIdType.MESH
F32 = jnp.float32
BF16 = jnp.bfloat16

BLK = 128
LIMIT = 16 << 20
GROUP = 16
XN, YN, ZH = 4, 4, 2
QUAD = 4


def dot(a, b, dims):
    return lax.dot_general(a, b, (dims, ((), ())), preferred_element_type=F32)


def terms_kernel(
    brow_hbm, bcol_hbm, live, obs_hbm, row_hbm, col_hbm, row_out, col_out, row_own, col_own,
    brow, bcol, row_t, col_t, obs, row_tab, row_acc, col_acc, arg_sems, sems,
):
    slots = obs.shape[0]
    n_row, n_col = row_acc.shape[0], col_acc.shape[0]

    args = [
        pltpu.make_async_copy(source, target, arg_sems.at[k])
        for k, (source, target) in enumerate(
            ((brow_hbm, brow), (bcol_hbm, bcol), (row_hbm, row_t), (col_hbm, col_t))
        )
    ]

    def fetch(g):
        part = pl.ds(g * GROUP, GROUP)
        return pltpu.make_async_copy(obs_hbm.at[part], obs.at[part], sems.at[g])

    for arg in args:
        arg.start()
    for g in range(slots // GROUP):
        fetch(g).start()
    row_acc[...] = jnp.zeros_like(row_acc)
    col_acc[...] = jnp.zeros_like(col_acc)
    for arg in args:
        arg.wait()
    for i in range(n_row):
        row_tab[i] = row_t[:, i * BLK : (i + 1) * BLK].T
    count = live[0, 0]

    def pick(k):
        i, j = brow[0, k], bcol[0, k]
        rt = row_t[:, pl.ds(pl.multiple_of(i * BLK, BLK), BLK)]
        ct = col_t[:, pl.ds(pl.multiple_of(j * BLK, BLK), BLK)]
        return i, j, rt, ct

    def group(g, carry):
        fetch(g).wait()

        @pl.when(g * GROUP < count)
        def _():
            for u in range(GROUP):
                k = g * GROUP + u
                i, _, _, ct = pick(k)
                res = dot(row_tab[i], ct, ((1,), (0,))) - obs[k].astype(F32)
                obs[k] = jnp.where(k < count, res, 0.0).astype(BF16)
            terms = []
            for u in range(GROUP):
                k = g * GROUP + u
                i, j, rt, ct = pick(k)
                res = obs[k]
                terms.append((i, j, dot(ct, res, ((1,), (1,))), dot(rt, res, ((1,), (0,)))))
            for i, j, row_term, col_term in terms:
                row_acc[i] += row_term
                col_acc[j] += col_term

        return carry

    lax.fori_loop(0, slots // GROUP, group, 0)
    row_out[...] = row_acc[...].astype(BF16)
    col_out[...] = col_acc[...].astype(BF16)

    src, rcv = lax.axis_index("src"), lax.axis_index("rcv")
    mine = rcv % 2 * (n_row // 2) + rcv // 2 * 2
    for u in range(2):
        part = pl.ds(pl.multiple_of((mine + u) * BLK, BLK), BLK)
        row_own[u] = 0.9 * row_t[:, part].astype(F32)
    part = pl.ds(pl.multiple_of(src // ZH * BLK, BLK), BLK)
    col_own[0] = 0.9 * col_t[:, part].astype(F32)


def sum_kernel(
    row_step, col_step, row_in, col_in, row_own, col_own, row_out, col_out,
    core_buf, far_sum, near_sum, far_buf, near_buf, far_send, far_recv, col_buf, col_send, col_recv,
    twin_in, send_sems, recv_sems,
):
    src, rcv = lax.axis_index("src"), lax.axis_index("rcv")
    x, y, zh = src // (YN * ZH), src // ZH % YN, src % ZH
    z, c = rcv // 2, rcv % 2
    q, p = z // QUAD, z % QUAD
    b = src // ZH
    half = row_in.shape[0] // 2
    qb = half // 2

    def at(zz, cc):
        return (src, zz * 2 + cc)

    core = at(z, 1 - c)
    far_z = (1 - q) * QUAD + p
    far = at(far_z, c)
    up = [q * QUAD + (p + d) % QUAD for d in range(1, QUAD)]
    down = [(p + QUAD - d) % QUAD for d in range(1, QUAD)]
    mates = [at(m, c) for m in up]
    steps = [(dx, dy) for dx in range(XN) for dy in range(YN) if dx or dy]
    steps.sort(key=lambda s: -(min(s[0], XN - s[0]) + min(s[1], YN - s[1])))
    places = [(x + dx) % XN * YN + (y + dy) % YN for dx, dy in steps]
    peers = [(place * ZH + zh, rcv) for place in places]
    twin = (b * ZH + 1 - zh, rcv)
    side = (b * ZH + 1 - zh, far_z * 2 + c)

    barrier = pltpu.get_barrier_semaphore()
    everyone = [core, far, side] + mates + peers
    for device in everyone:
        pl.semaphore_signal(barrier, inc=1, device_id=device, device_id_type=MESH)
    pl.semaphore_wait(barrier, len(everyone))
    pl.semaphore_signal(twin_in, inc=1, device_id=far, device_id_type=MESH)

    sent = []

    def copy(source, target, number, device):
        return pltpu.make_async_remote_copy(
            src_ref=source, dst_ref=target, send_sem=send_sems.at[number], recv_sem=recv_sems.at[number],
            device_id=device, device_id_type=MESH,
        )

    def send(source, target, number, device):
        one = copy(source, target, number, device)
        one.start()
        sent.append(one)
        return one

    def leave(ones):
        for one in ones:
            one.wait_send()
        sent[:] = [one for one in sent if not any(one is other for other in ones)]

    def arrive(target, number):
        copy(target, target, number, core).wait_recv()

    CORE_FAR, CORE_NEAR, FAR_IN, NEAR_IN, FAR, COL_IN, TWIN = 0, 8, 9, 15, 18, 20, 35
    NEAR_OUT, FAR_OUT, RELAY, CORE_OUT, COL_OUT = 36, 39, 41, 47, 59

    def far_block(h, d):
        return ((1 - q) * QUAD + (p + d + 1) % QUAD) * 2 + h

    for h in range(2):
        for d in range(QUAD):
            k = h * QUAD + d
            send(row_in.at[(1 - c) * half + far_block(h, d)], core_buf.at[0, k], CORE_FAR + k, core)
    send(row_in.at[pl.ds((1 - c) * half + q * qb, qb)], core_buf.at[1], CORE_NEAR, core)
    for k, (place, peer) in enumerate(zip(places, peers)):
        send(col_in.at[place], col_buf.at[k], COL_IN + k, peer)

    first = []
    for h in range(2):
        for d in range(QUAD):
            k = h * QUAD + d
            arrive(core_buf.at[0, k], CORE_FAR + k)
            own = row_in[c * half + far_block(h, d)].astype(F32)
            far_sum[k] = (own + core_buf[0, k].astype(F32)).astype(BF16)
            if d < QUAD - 1:
                first.append(send(far_sum.at[k], far_buf.at[d, h], FAR_IN + d * 2 + h, mates[d]))
    arrive(core_buf.at[1], CORE_NEAR)
    own = row_in[pl.ds(c * half + q * qb, qb)].astype(F32)
    near_sum[...] = (own + core_buf[1].astype(F32)).astype(BF16)

    for h in range(2):
        acc = far_sum[h * QUAD + QUAD - 1].astype(F32)
        for d in range(QUAD - 1):
            arrive(far_buf.at[d, h], FAR_IN + d * 2 + h)
            acc += far_buf[d, h].astype(F32)
        far_send[h] = acc.astype(BF16)
        send(far_send.at[h], far_recv.at[h], FAR + h, far)
        if h == 0:
            leave(first)
            for d in range(QUAD - 1):
                part = pl.ds((p + d + 1) % QUAD * 2, 2)
                send(near_sum.at[part], near_buf.at[d], NEAR_IN + d, mates[d])

    acc = col_in[b].astype(F32)
    for k in range(len(peers)):
        arrive(col_buf.at[k], COL_IN + k)
        acc += col_buf[k].astype(F32)
    col_send[...] = acc.astype(BF16)
    pl.semaphore_wait(twin_in, 1)
    send(col_send, col_recv, TWIN, twin)

    near = near_sum[pl.ds(p * 2, 2)].astype(F32)
    for d in range(QUAD - 1):
        arrive(near_buf.at[d], NEAR_IN + d)
        near += near_buf[d].astype(F32)

    def blocks(zz, cc):
        return row_out.at[pl.ds(cc * half + zz * 2, 2)]

    mine = blocks(z, c)
    first = []
    for h in range(2):
        arrive(far_recv.at[h], FAR + h)
        acc = near[h] + far_recv[h].astype(F32)
        mine[h] = (row_own[h] - row_step * acc).astype(BF16)
        first.append(send(mine.at[h], mine.at[h], FAR_OUT + h, far))
    leave(first)
    for d in range(QUAD - 1):
        send(mine, mine, NEAR_OUT + d, mates[d])
    send(mine, mine, CORE_OUT, core)

    arrive(col_recv, TWIN)
    acc = col_send[...].astype(F32) + col_recv[...].astype(F32)
    col_out[b] = (col_own[0] - col_step * acc).astype(BF16)
    for k, peer in enumerate(peers):
        send(col_out.at[b], col_out.at[b], COL_OUT + k, peer)

    parts = [blocks(z, 1 - c)]

    def share(view):
        one = view(c)
        send(one, one, CORE_OUT + len(parts), core)
        parts.append(view(1 - c))

    for h in range(2):
        one = blocks(far_z, c).at[h]
        arrive(one, FAR_OUT + h)
        for d in range(QUAD - 1):
            send(one, one, RELAY + h * 3 + d, mates[d])
        share(lambda cc: blocks(far_z, cc).at[h])
    for d in range(QUAD - 1):
        spot = q * QUAD + down[d]
        arrive(blocks(spot, c), NEAR_OUT + d)
        share(lambda cc: blocks(spot, cc))
    for h in range(2):
        for d in range(QUAD - 1):
            spot = (1 - q) * QUAD + down[d]
            arrive(blocks(spot, c).at[h], RELAY + h * 3 + d)
            share(lambda cc: blocks(spot, cc).at[h])
    for k, (dx, dy) in enumerate(steps):
        place = (x + XN - dx) % XN * YN + (y + YN - dy) % YN
        arrive(col_out.at[place], COL_OUT + k)
    for k, part in enumerate(parts):
        arrive(part, CORE_OUT + k)
    for one in sent:
        one.wait_send()


def local(observed, block_row, block_col, live, row_factor, col_factor):
    slot_data = observed[0]
    slots = slot_data.shape[0]
    rank = row_factor.shape[1]
    n_row, n_col = row_factor.shape[0] // BLK, col_factor.shape[0] // BLK
    row_t, col_t = row_factor.T, col_factor.T
    vmem = pl.BlockSpec(memory_space=pltpu.VMEM)
    hbm = pl.BlockSpec(memory_space=pl.ANY)

    fixed = functools.partial(pltpu.with_memory_space_constraint, memory_space=pltpu.HBM)
    row_terms, col_terms, row_own, col_own = pl.pallas_call(
        terms_kernel,
        out_shape=(
            jax.ShapeDtypeStruct((n_row, rank, BLK), BF16),
            jax.ShapeDtypeStruct((n_col, rank, BLK), BF16),
            jax.ShapeDtypeStruct((2, rank, BLK), F32),
            jax.ShapeDtypeStruct((1, rank, BLK), F32),
        ),
        in_specs=[hbm, hbm, pl.BlockSpec(memory_space=pltpu.SMEM), hbm, hbm, hbm],
        out_specs=(vmem,) * 4,
        scratch_shapes=[
            pltpu.SMEM((1, slots), jnp.int32),
            pltpu.SMEM((1, slots), jnp.int32),
            pltpu.VMEM((rank, n_row * BLK), BF16),
            pltpu.VMEM((rank, n_col * BLK), BF16),
            pltpu.VMEM((slots, BLK, BLK), BF16),
            pltpu.VMEM((n_row, BLK, rank), BF16),
            pltpu.VMEM((n_row, rank, BLK), F32),
            pltpu.VMEM((n_col, rank, BLK), F32),
            pltpu.SemaphoreType.DMA((4,)),
            pltpu.SemaphoreType.DMA((slots // GROUP,)),
        ],
        compiler_params=pltpu.CompilerParams(vmem_limit_bytes=LIMIT),
        name="terms",
    )(fixed(block_row), fixed(block_col), live, fixed(slot_data), fixed(row_t), fixed(col_t))

    row_step = 0.5 / math.sqrt(slots * BLK * lax.axis_size("rcv") // n_row)
    col_step = 0.5 / math.sqrt(slots * BLK * lax.axis_size("src") // n_col)
    copies = 74
    new_rows, new_cols = pl.pallas_call(
        functools.partial(sum_kernel, row_step, col_step),
        out_shape=(
            jax.ShapeDtypeStruct((n_row, rank, BLK), BF16),
            jax.ShapeDtypeStruct((n_col, rank, BLK), BF16),
        ),
        in_specs=[vmem] * 4,
        out_specs=(vmem, vmem),
        scratch_shapes=[
            pltpu.VMEM((2, n_row // 4, rank, BLK), BF16),
            pltpu.VMEM((n_row // 4, rank, BLK), BF16),
            pltpu.VMEM((n_row // 4, rank, BLK), BF16),
            pltpu.VMEM((QUAD - 1, 2, rank, BLK), BF16),
            pltpu.VMEM((QUAD - 1, 2, rank, BLK), BF16),
            pltpu.VMEM((2, rank, BLK), BF16),
            pltpu.VMEM((2, rank, BLK), BF16),
            pltpu.VMEM((XN * YN - 1, rank, BLK), BF16),
            pltpu.VMEM((rank, BLK), BF16),
            pltpu.VMEM((rank, BLK), BF16),
            pltpu.SemaphoreType.REGULAR,
            pltpu.SemaphoreType.DMA((copies,)),
            pltpu.SemaphoreType.DMA((copies,)),
        ],
        compiler_params=pltpu.CompilerParams(
            collective_id=0, has_side_effects=True, vmem_limit_bytes=LIMIT
        ),
        name="sums",
    )(row_terms, col_terms, row_own, col_own)

    def whole(blocks):
        return blocks.transpose(1, 0, 2).reshape(rank, -1).T

    return whole(new_rows), whole(new_cols)


def solution(mesh):
    return jax.shard_map(
        local,
        mesh=mesh,
        in_specs=(
            P("src", "rcv", None, None),
            P("src", "rcv"),
            P("src", "rcv"),
            P("src", "rcv"),
            P("src", None),
            P("rcv", None),
        ),
        out_specs=(P("src", None), P("rcv", None)),
        check_vma=False,
    )
```

```python
import functools
import math

import jax
import jax.numpy as jnp
from jax import lax
from jax.experimental import pallas as pl
from jax.experimental.pallas import tpu as pltpu
from jax.sharding import PartitionSpec as P

MESH = pl.DeviceIdType.MESH
F32 = jnp.float32
BF16 = jnp.bfloat16

BLK = 128
LIMIT = 16 << 20
GROUP = 16
XN, YN, ZH = 4, 4, 2
QUAD = 4


def dot(a, b, dims):
    return lax.dot_general(a, b, (dims, ((), ())), preferred_element_type=F32)


def terms_kernel(
    brow_hbm, bcol_hbm, live, obs_hbm, row_hbm, col_hbm, row_out, col_out, row_own, col_own,
    brow, bcol, row_t, col_t, obs, row_tab, row_acc, col_acc, arg_sems, sems,
):
    slots = obs.shape[0]
    n_row, n_col = row_acc.shape[0], col_acc.shape[0]

    args = [
        pltpu.make_async_copy(source, target, arg_sems.at[k])
        for k, (source, target) in enumerate(
            ((brow_hbm, brow), (bcol_hbm, bcol), (row_hbm, row_t), (col_hbm, col_t))
        )
    ]

    def fetch(g):
        part = pl.ds(g * GROUP, GROUP)
        return pltpu.make_async_copy(obs_hbm.at[part], obs.at[part], sems.at[g])

    for arg in args:
        arg.start()
    for g in range(slots // GROUP):
        fetch(g).start()
    row_acc[...] = jnp.zeros_like(row_acc)
    col_acc[...] = jnp.zeros_like(col_acc)
    for arg in args:
        arg.wait()
    for i in range(n_row):
        row_tab[i] = row_t[:, i * BLK : (i + 1) * BLK].T
    count = live[0, 0]

    def pick(k):
        i, j = brow[0, k], bcol[0, k]
        rt = row_t[:, pl.ds(pl.multiple_of(i * BLK, BLK), BLK)]
        ct = col_t[:, pl.ds(pl.multiple_of(j * BLK, BLK), BLK)]
        return i, j, rt, ct

    def group(g, carry):
        fetch(g).wait()

        @pl.when(g * GROUP < count)
        def _():
            for u in range(GROUP):
                k = g * GROUP + u
                i, _, _, ct = pick(k)
                res = dot(row_tab[i], ct, ((1,), (0,))) - obs[k].astype(F32)
                obs[k] = jnp.where(k < count, res, 0.0).astype(BF16)
            terms = []
            for u in range(GROUP):
                k = g * GROUP + u
                i, j, rt, ct = pick(k)
                res = obs[k]
                terms.append((i, j, dot(ct, res, ((1,), (1,))), dot(rt, res, ((1,), (0,)))))
            for i, j, row_term, col_term in terms:
                row_acc[i] += row_term
                col_acc[j] += col_term

        return carry

    lax.fori_loop(0, slots // GROUP, group, 0)
    row_out[...] = row_acc[...].astype(BF16)
    col_out[...] = col_acc[...].astype(BF16)

    src, rcv = lax.axis_index("src"), lax.axis_index("rcv")
    mine = rcv % 2 * (n_row // 2) + rcv // 2 * 2
    for u in range(2):
        part = pl.ds(pl.multiple_of((mine + u) * BLK, BLK), BLK)
        row_own[u] = 0.9 * row_t[:, part].astype(F32)
    part = pl.ds(pl.multiple_of(src // ZH * BLK, BLK), BLK)
    col_own[0] = 0.9 * col_t[:, part].astype(F32)


def sum_kernel(
    row_step, col_step, row_in, col_in, row_own, col_own, row_out, col_out,
    core_buf, far_sum, near_sum, far_buf, near_buf, far_send, far_recv, col_buf, col_send, col_recv,
    twin_in, send_sems, recv_sems,
):
    src, rcv = lax.axis_index("src"), lax.axis_index("rcv")
    x, y, zh = src // (YN * ZH), src // ZH % YN, src % ZH
    z, c = rcv // 2, rcv % 2
    q, p = z // QUAD, z % QUAD
    b = src // ZH
    half = row_in.shape[0] // 2
    qb = half // 2

    def at(zz, cc):
        return (src, zz * 2 + cc)

    core = at(z, 1 - c)
    far_z = (1 - q) * QUAD + p
    far = at(far_z, c)
    up = [q * QUAD + (p + d) % QUAD for d in range(1, QUAD)]
    down = [(p + QUAD - d) % QUAD for d in range(1, QUAD)]
    mates = [at(m, c) for m in up]
    steps = [(dx, dy) for dx in range(XN) for dy in range(YN) if dx or dy]
    steps.sort(key=lambda s: -(min(s[0], XN - s[0]) + min(s[1], YN - s[1])))
    places = [(x + dx) % XN * YN + (y + dy) % YN for dx, dy in steps]
    peers = [(place * ZH + zh, rcv) for place in places]
    twin = (b * ZH + 1 - zh, rcv)
    side = (b * ZH + 1 - zh, far_z * 2 + c)

    barrier = pltpu.get_barrier_semaphore()
    everyone = [core, far, side] + mates + peers
    for device in everyone:
        pl.semaphore_signal(barrier, inc=1, device_id=device, device_id_type=MESH)
    pl.semaphore_wait(barrier, len(everyone))
    pl.semaphore_signal(twin_in, inc=1, device_id=far, device_id_type=MESH)

    sent = []

    def copy(source, target, number, device):
        return pltpu.make_async_remote_copy(
            src_ref=source, dst_ref=target, send_sem=send_sems.at[number], recv_sem=recv_sems.at[number],
            device_id=device, device_id_type=MESH,
        )

    def send(source, target, number, device):
        one = copy(source, target, number, device)
        one.start()
        sent.append(one)
        return one

    def leave(ones):
        for one in ones:
            one.wait_send()
        sent[:] = [one for one in sent if not any(one is other for other in ones)]

    def arrive(target, number):
        copy(target, target, number, core).wait_recv()

    CORE_FAR, CORE_NEAR, FAR_IN, NEAR_IN, FAR, COL_IN, TWIN = 0, 8, 9, 15, 18, 20, 35
    NEAR_OUT, FAR_OUT, RELAY, CORE_OUT, COL_OUT = 36, 39, 41, 47, 59

    def far_block(h, d):
        return ((1 - q) * QUAD + (p + d + 1) % QUAD) * 2 + h

    for h in range(2):
        for d in range(QUAD):
            k = h * QUAD + d
            send(row_in.at[(1 - c) * half + far_block(h, d)], core_buf.at[0, k], CORE_FAR + k, core)
    send(row_in.at[pl.ds((1 - c) * half + q * qb, qb)], core_buf.at[1], CORE_NEAR, core)
    for k, (place, peer) in enumerate(zip(places, peers)):
        send(col_in.at[place], col_buf.at[k], COL_IN + k, peer)

    first = []
    for h in range(2):
        for d in range(QUAD):
            k = h * QUAD + d
            arrive(core_buf.at[0, k], CORE_FAR + k)
            own = row_in[c * half + far_block(h, d)].astype(F32)
            far_sum[k] = (own + core_buf[0, k].astype(F32)).astype(BF16)
            if d < QUAD - 1:
                first.append(send(far_sum.at[k], far_buf.at[d, h], FAR_IN + d * 2 + h, mates[d]))
    arrive(core_buf.at[1], CORE_NEAR)
    own = row_in[pl.ds(c * half + q * qb, qb)].astype(F32)
    near_sum[...] = (own + core_buf[1].astype(F32)).astype(BF16)

    for h in range(2):
        acc = far_sum[h * QUAD + QUAD - 1].astype(F32)
        for d in range(QUAD - 1):
            arrive(far_buf.at[d, h], FAR_IN + d * 2 + h)
            acc += far_buf[d, h].astype(F32)
        far_send[h] = acc.astype(BF16)
        send(far_send.at[h], far_recv.at[h], FAR + h, far)
        if h == 0:
            leave(first)
            for d in range(QUAD - 1):
                part = pl.ds((p + d + 1) % QUAD * 2, 2)
                send(near_sum.at[part], near_buf.at[d], NEAR_IN + d, mates[d])

    acc = col_in[b].astype(F32)
    for k in range(len(peers)):
        arrive(col_buf.at[k], COL_IN + k)
        acc += col_buf[k].astype(F32)
    col_send[...] = acc.astype(BF16)
    pl.semaphore_wait(twin_in, 1)
    send(col_send, col_recv, TWIN, twin)

    near = near_sum[pl.ds(p * 2, 2)].astype(F32)
    for d in range(QUAD - 1):
        arrive(near_buf.at[d], NEAR_IN + d)
        near += near_buf[d].astype(F32)

    def lanes(out, block, count=1):
        return out.at[:, pl.ds(pl.multiple_of(block * BLK, BLK), count * BLK)]

    def pair(zz, cc):
        return lanes(row_out, cc * half + zz * 2, 2)

    def single(zz, cc, h):
        return lanes(row_out, cc * half + zz * 2 + h)

    mine = pair(z, c)
    first = []
    for h in range(2):
        arrive(far_recv.at[h], FAR + h)
        acc = near[h] + far_recv[h].astype(F32)
        one = single(z, c, h)
        one[...] = (row_own[h] - row_step * acc).astype(BF16)
        first.append(send(one, one, FAR_OUT + h, far))
    leave(first)
    for d in range(QUAD - 1):
        send(mine, mine, NEAR_OUT + d, mates[d])
    send(mine, mine, CORE_OUT, core)

    arrive(col_recv, TWIN)
    acc = col_send[...].astype(F32) + col_recv[...].astype(F32)
    col_mine = lanes(col_out, b)
    col_mine[...] = (col_own[0] - col_step * acc).astype(BF16)
    for k, peer in enumerate(peers):
        send(col_mine, col_mine, COL_OUT + k, peer)

    parts = [pair(z, 1 - c)]

    def share(view):
        one = view(c)
        send(one, one, CORE_OUT + len(parts), core)
        parts.append(view(1 - c))

    for h in range(2):
        one = single(far_z, c, h)
        arrive(one, FAR_OUT + h)
        for d in range(QUAD - 1):
            send(one, one, RELAY + h * 3 + d, mates[d])
        share(lambda cc: single(far_z, cc, h))
    for d in range(QUAD - 1):
        spot = q * QUAD + down[d]
        arrive(pair(spot, c), NEAR_OUT + d)
        share(lambda cc: pair(spot, cc))
    for h in range(2):
        for d in range(QUAD - 1):
            spot = (1 - q) * QUAD + down[d]
            arrive(single(spot, c, h), RELAY + h * 3 + d)
            share(lambda cc: single(spot, cc, h))
    for k, (dx, dy) in enumerate(steps):
        place = (x + XN - dx) % XN * YN + (y + YN - dy) % YN
        arrive(lanes(col_out, place), COL_OUT + k)
    for k, part in enumerate(parts):
        arrive(part, CORE_OUT + k)
    for one in sent:
        one.wait_send()


def local(observed, block_row, block_col, live, row_factor, col_factor):
    slot_data = observed[0]
    slots = slot_data.shape[0]
    rank = row_factor.shape[1]
    n_row, n_col = row_factor.shape[0] // BLK, col_factor.shape[0] // BLK
    row_t, col_t = row_factor.T, col_factor.T
    vmem = pl.BlockSpec(memory_space=pltpu.VMEM)
    hbm = pl.BlockSpec(memory_space=pl.ANY)

    fixed = functools.partial(pltpu.with_memory_space_constraint, memory_space=pltpu.HBM)
    row_terms, col_terms, row_own, col_own = pl.pallas_call(
        terms_kernel,
        out_shape=(
            jax.ShapeDtypeStruct((n_row, rank, BLK), BF16),
            jax.ShapeDtypeStruct((n_col, rank, BLK), BF16),
            jax.ShapeDtypeStruct((2, rank, BLK), F32),
            jax.ShapeDtypeStruct((1, rank, BLK), F32),
        ),
        in_specs=[hbm, hbm, pl.BlockSpec(memory_space=pltpu.SMEM), hbm, hbm, hbm],
        out_specs=(vmem,) * 4,
        scratch_shapes=[
            pltpu.SMEM((1, slots), jnp.int32),
            pltpu.SMEM((1, slots), jnp.int32),
            pltpu.VMEM((rank, n_row * BLK), BF16),
            pltpu.VMEM((rank, n_col * BLK), BF16),
            pltpu.VMEM((slots, BLK, BLK), BF16),
            pltpu.VMEM((n_row, BLK, rank), BF16),
            pltpu.VMEM((n_row, rank, BLK), F32),
            pltpu.VMEM((n_col, rank, BLK), F32),
            pltpu.SemaphoreType.DMA((4,)),
            pltpu.SemaphoreType.DMA((slots // GROUP,)),
        ],
        compiler_params=pltpu.CompilerParams(vmem_limit_bytes=LIMIT),
        name="terms",
    )(fixed(block_row), fixed(block_col), live, fixed(slot_data), fixed(row_t), fixed(col_t))

    row_step = 0.5 / math.sqrt(slots * BLK * lax.axis_size("rcv") // n_row)
    col_step = 0.5 / math.sqrt(slots * BLK * lax.axis_size("src") // n_col)
    copies = 74
    new_rows, new_cols = pl.pallas_call(
        functools.partial(sum_kernel, row_step, col_step),
        out_shape=(
            jax.ShapeDtypeStruct((rank, n_row * BLK), BF16),
            jax.ShapeDtypeStruct((rank, n_col * BLK), BF16),
        ),
        in_specs=[vmem] * 4,
        out_specs=(vmem, vmem),
        scratch_shapes=[
            pltpu.VMEM((2, n_row // 4, rank, BLK), BF16),
            pltpu.VMEM((n_row // 4, rank, BLK), BF16),
            pltpu.VMEM((n_row // 4, rank, BLK), BF16),
            pltpu.VMEM((QUAD - 1, 2, rank, BLK), BF16),
            pltpu.VMEM((QUAD - 1, 2, rank, BLK), BF16),
            pltpu.VMEM((2, rank, BLK), BF16),
            pltpu.VMEM((2, rank, BLK), BF16),
            pltpu.VMEM((XN * YN - 1, rank, BLK), BF16),
            pltpu.VMEM((rank, BLK), BF16),
            pltpu.VMEM((rank, BLK), BF16),
            pltpu.SemaphoreType.REGULAR,
            pltpu.SemaphoreType.DMA((copies,)),
            pltpu.SemaphoreType.DMA((copies,)),
        ],
        compiler_params=pltpu.CompilerParams(
            collective_id=0, has_side_effects=True, vmem_limit_bytes=LIMIT
        ),
        name="sums",
    )(row_terms, col_terms, row_own, col_own)

    return new_rows.T, new_cols.T


def solution(mesh):
    return jax.shard_map(
        local,
        mesh=mesh,
        in_specs=(
            P("src", "rcv", None, None),
            P("src", "rcv"),
            P("src", "rcv"),
            P("src", "rcv"),
            P("src", None),
            P("rcv", None),
        ),
        out_specs=(P("src", None), P("rcv", None)),
        check_vma=False,
    )
```
